256 devices in a mesh: tile: 32 (over y_hi, z, core), seg: 8 (over x, y_lo).
Axes of the slice: x: 4, y: 4 (y_hi: 2, y_lo: 2; y = y_hi * 2 + y_lo), z: 8, core: 2. Of those that a mesh axis runs over, the one named last changes fastest.
Arguments:
- right_sides: float32 [524288, 512], P(('tile', 'seg')), may hold values from -6 to 6
- leaf_proj: float32 [32, 128, 64, 128], P('tile', 'seg'), may hold values from -0.5 to 0.5
- col_levels: float32 [32, 4, 64, 128, 128], P('tile', None, 'seg'), may hold values from -0.5 to 0.5
- middle_factor: float32 [32, 128, 64, 64], P('tile', 'seg'), may hold values from -0.75 to 0.75
- row_levels: float32 [32, 4, 64, 128, 128], P('tile', None, 'seg'), may hold values from -0.5 to 0.5
- leaf_expand: float32 [32, 128, 128, 64], P('tile', 'seg'), may hold values from -0.125 to 0.125
Outputs:
- product: float32 [16384, 512], P(('seg', 'tile'))
The draws below stay inside these ranges and needn't reach their ends.
All inputs are finite; a program needn't handle non-finite values.
Results may differ from the reference program's by a relative error of at most 0.0001.
Values sent between devices are 32-bit elements; how exact they have to be, the bound alone decides.
A program may use at most 64 MiB of HBM per device.

```python
import jax
import jax.numpy as jnp
from jax import lax

K = 64
LEAF = 128
LVL = 4
R = 512
BOX = 16
TILES = 32
LEAVES = 128
PAIRS = 64
C = 16384
COLS = 524288
N_TILE = 32
N_SEG = 8


def block_levels(key, dims, cuts, low, top_value):
    loudness = 1.0
    for dim, shards_of in cuts:
        draws = jax.random.uniform(jax.random.fold_in(jax.random.fold_in(key, 6), dim), (shards_of,), jnp.float32, low / len(cuts), top_value / len(cuts))
        loudness = loudness * jnp.repeat(jnp.exp(draws), dims[dim] // shards_of).reshape((-1,) + (1,) * (len(dims) - 1 - dim))
    return loudness


def bell_draw(own_key, dims, scale, reach, cuts=(), dtype=jnp.bfloat16):
    array = jax.random.normal(own_key, dims, jnp.float32) * scale
    if len(cuts) > 0:
        array = block_levels(own_key, dims, cuts, -0.22, 0.18) * array
    return jnp.clip(array, min=-reach, max=reach).astype(dtype)


def setup_inputs(seed: int = 0) -> dict:
    seeds = jax.random.split(jax.random.key(seed), 7)
    return {
        "right_sides": bell_draw(seeds[0], (COLS, R), 1.0, 6.0, ((0, 256),), jnp.float32),
        "leaf_proj": bell_draw(seeds[1], (TILES, LEAVES, K, LEAF), LEAF ** -0.5, 0.5, ((0, 32), (1, 8)), jnp.float32),
        "col_levels": bell_draw(seeds[2], (TILES, LVL, PAIRS, 2 * K, 2 * K), (2 * K) ** -0.5, 0.5, ((0, 32), (2, 8)), jnp.float32),
        "middle_factor": bell_draw(seeds[3], (TILES, LEAVES, K, K), K ** -0.5, 0.75, ((0, 32), (1, 8)), jnp.float32),
        "row_levels": bell_draw(seeds[4], (TILES, LVL, PAIRS, 2 * K, 2 * K), (2 * K) ** -0.5, 0.5, ((0, 32), (2, 8)), jnp.float32),
        "leaf_expand": bell_draw(seeds[5], (TILES, LEAVES, LEAF, K), (K * N_TILE) ** -0.5, 0.125, ((0, 32), (1, 8)), jnp.float32),
    }


def levels(coeffs, weights, groups):
    for level in range(LVL):
        stride = 2 ** level
        blocks = BOX // (2 * stride)
        wide = weights[level].reshape(groups, blocks, stride, 2, K, 2, K)
        split = coeffs.reshape(groups, blocks, 2, stride, K, R)
        mixed = jnp.einsum('gaeuvwx,gawexr->gauevr', wide, split, precision=lax.Precision.HIGHEST)
        coeffs = mixed.reshape(groups, BOX, K, R)
    return coeffs


def one_tile(columns, proj, col_weights, middle, row_weights, expand):
    coeffs = jnp.einsum('nkl,nlr->nkr', proj, columns.reshape(LEAVES, LEAF, R), precision=lax.Precision.HIGHEST)
    coeffs = levels(coeffs.reshape(N_SEG, BOX, K, R), col_weights, N_SEG)
    coeffs = jnp.einsum('nkj,njr->nkr', middle, coeffs.reshape(LEAVES, K, R), precision=lax.Precision.HIGHEST)
    coeffs = coeffs.reshape(N_SEG, N_SEG, BOX // N_SEG, K, R).transpose(1, 0, 2, 3, 4).reshape(N_SEG, BOX, K, R)
    coeffs = levels(coeffs, row_weights, N_SEG)
    rows = jnp.einsum('nlk,nkr->nlr', expand, coeffs.reshape(LEAVES, K, R), precision=lax.Precision.HIGHEST)
    return rows.reshape(C, R)


def reference(right_sides, leaf_proj, col_levels, middle_factor, row_levels, leaf_expand):
    def add_tile(total, pieces):
        return total + one_tile(*pieces), None

    stacked = (right_sides.reshape(TILES, C, R), leaf_proj, col_levels, middle_factor, row_levels, leaf_expand)
    total, _ = lax.scan(add_tile, jnp.zeros((C, R), jnp.float32), stacked)
    return total
```

```python
import functools

import jax
import jax.numpy as jnp
from jax import lax
from jax.experimental import pallas as pl
from jax.experimental.pallas import tpu as pltpu
from jax.sharding import PartitionSpec as P

K = 64
LEAF = 128
BOX = 16
R = 512
C = 4
W = R // C
ROWS = BOX * LEAF
F32 = jnp.float32
BF16 = jnp.bfloat16
MESH = pl.DeviceIdType.MESH
PEERS = ((2, 1), (1, 1), (3, 1), (2, 0), (1, 0), (3, 0), (0, 1))


def halves(v):
    hi = v.astype(BF16)
    return hi, (v - hi.astype(F32)).astype(BF16)


def wide(v):
    return jnp.concatenate(halves(v), axis=1)


def product(weight, hl):
    r = jnp.dot(weight, jnp.concatenate([hl, hl], axis=0), preferred_element_type=F32)
    n = r.shape[1] // 2
    return r[:, :n] + r[:, n:]


def exact(a, b):
    hl = wide(b)
    ahi, alo = halves(a)
    r = jnp.dot(ahi, hl, preferred_element_type=F32) + jnp.dot(alo, hl, preferred_element_type=F32)
    n = r.shape[1] // 2
    return r[:, :n] + r[:, n:]


def level(l, weights, src, dst):
    d = 2**l
    for a in range(BOX // (2 * d)):
        for e in range(d):
            p, j = a * 2 * d + e, a * d + e
            y = product(weights[j], jnp.concatenate([src[p], src[p + d]], axis=0))
            dst[p] = wide(y[:K])
            dst[p + d] = wide(y[K:])


def kernel(
    x_hbm, proj_hbm, col_hbm, mid_hbm, row_hbm, exp_hbm, out,
    xbuf, proj, col, mid, row, expt,
    wproj, wcol, wrow, wend, hla, hlb,
    coef, got, own, pair, rp, rm, fin, ysend, yrecv,
    lsem, asend, arecv, csem, dsend, drecv, psend, precv, msend, mrecv, ysems, yrecvs,
):
    tile, seg = lax.axis_index("tile"), lax.axis_index("seg")
    core, z, yh = tile % 2, (tile // 2) % 8, tile // 16
    xx, yl = seg // 2, seg % 2

    def at(core=core, z=z, yh=yh, xx=xx, yl=yl):
        return ((yh * 8 + z) * 2 + core, xx * 2 + yl)

    other = at(core=1 - core)
    zup, zdown = at(z=(z + 1) % 8), at(z=(z + 7) % 8)
    far = at(yh=1 - yh)
    peers = [at(xx=(xx + dx) % 4, yl=(yl + dy) % 2) for dx, dy in PEERS]

    barrier = pltpu.get_barrier_semaphore()
    friends = peers + [other, zup, zdown, far]
    for f in friends:
        pl.semaphore_signal(barrier, inc=1, device_id=f, device_id_type=MESH)

    def xcopy(c):
        lanes = pl.ds(pl.multiple_of(c * W, W), W)
        return pltpu.make_async_copy(x_hbm.at[:, lanes], xbuf.at[c], lsem.at[c])

    loads = [
        pltpu.make_async_copy(src.at[0], dst, lsem.at[C + i])
        for i, (src, dst) in enumerate(
            ((proj_hbm, proj), (col_hbm, col), (mid_hbm, mid), (row_hbm, row), (exp_hbm, expt))
        )
    ]
    loads[0].start()
    xcopy(0).start()
    loads[1].start()
    loads[2].start()
    for c in range(1, C):
        xcopy(c).start()
    loads[3].start()
    loads[4].start()

    def remote(src, dst, send, recv, to):
        return pltpu.make_async_remote_copy(
            src_ref=src, dst_ref=dst, send_sem=send, recv_sem=recv, device_id=to, device_id_type=MESH
        )

    def spread(c, k):
        to = peers[k]
        return remote(coef.at[c, to[1]], got.at[c, seg], asend.at[c, k], arecv.at[c, k], to)

    def keep(c):
        return pltpu.make_async_copy(coef.at[c, seg], got.at[c, seg], csem.at[c])

    def swap(c):
        return remote(own.at[c, 1 - core], pair.at[c], dsend.at[c], drecv.at[c], other)

    def up(c, src, slot):
        return remote(src, rp.at[c, slot], psend.at[c, slot], precv.at[c, slot], zup)

    def down(c, src, slot):
        return remote(src, rm.at[c, slot], msend.at[c, slot], mrecv.at[c, slot], zdown)

    def cross(c):
        return remote(ysend.at[c], yrecv.at[c], ysems.at[c], yrecvs.at[c], far)

    loads[0].wait()
    for n in range(BOX):
        wproj[n] = wide(proj[n])
    loads[1].wait()

    @pl.loop(0, 3)
    def _(l):
        for j in range(8):
            wcol[l, j] = wide(col[l, j])

    loads[2].wait()
    for j in range(8):
        wcol[3, j, :K] = wide(exact(mid[j], col[3, j, :K]))
        wcol[3, j, K:] = wide(exact(mid[j + 8], col[3, j, K:]))

    @pl.loop(0, C)
    def _(c):
        xcopy(c).wait()
        for n in range(BOX):
            hla[n] = wide(product(wproj[n], wide(xbuf[c, n * LEAF : (n + 1) * LEAF])))
        level(0, wcol.at[0], hla, hlb)
        level(1, wcol.at[1], hlb, hla)
        level(2, wcol.at[2], hla, hlb)
        for j in range(8):
            y = product(wcol[3, j], jnp.concatenate([hlb[j], hlb[j + 8]], axis=0))
            rows = slice((j % 2) * K, (j % 2) * K + K)
            coef[c, j // 2, rows] = y[:K]
            coef[c, j // 2 + 4, rows] = y[K:]

        @pl.when(c == 0)
        def _():
            pl.semaphore_wait(barrier, len(friends))

        for k in range(len(PEERS)):
            spread(c, k).start()
        keep(c).start()

    loads[3].wait()

    @pl.loop(0, 3)
    def _(l):
        for j in range(8):
            wrow[l, j] = wide(row[l, j])

    loads[4].wait()
    for j in range(8):
        wend[j, :LEAF] = wide(exact(expt[j].T, row[3, j, :K]))
        wend[j, LEAF:] = wide(exact(expt[j + 8].T, row[3, j, K:]))

    def begin(c):
        swap(c).wait_recv()
        for jj in (4, 3, 5, 2, 6, 1, 7, 0):
            zz = (z + jj) % 8
            for b in range(2):
                n = b * 8 + zz
                own[c, core, n] = own[c, core, n] + pair[c, n]
            if jj == 4:
                up(c, own.at[c, core, zz], 0).start()
                down(c, own.at[c, core, 8 + zz], 0).start()
            if jj == 3:
                up(c, own.at[c, core, 8 + zz], 2).start()
            if jj == 5:
                down(c, own.at[c, core, zz], 2).start()

    def chain(c, j):
        for e in range(1 if j == 3 else 2):
            here = {3: 0, 2: 1, 1: 3}[j] + e
            there = {3: 1, 2: 3, 1: 5}[j] + e
            up(c, rp.at[c, here], here).wait_recv()
            rp[c, here] = rp[c, here] + own[c, core, e * 8 + (z + j) % 8]
            up(c, rp.at[c, here], there).start()
            down(c, rm.at[c, here], here).wait_recv()
            rm[c, here] = rm[c, here] + own[c, core, (1 - e) * 8 + (z + 8 - j) % 8]
            down(c, rm.at[c, here], there).start()

    def arrive(c):
        for e in range(2):
            up(c, rp.at[c, 5 + e], 5 + e).wait_recv()
            down(c, rm.at[c, 5 + e], 5 + e).wait_recv()

        def total(b):
            return own[c, core, b * 8 + z] + rp[c, 5 + b] + rm[c, 6 - b]

        ysend[c] = total(1 - yh)
        cross(c).start()
        fin[c] = total(yh)

    def finish(c):
        cross(c).wait_recv()
        out[:, pl.ds(pl.multiple_of(c * W, W), W)] = fin[c] + yrecv[c]

    @pl.loop(0, C)
    def _(c):
        for k in range(len(PEERS)):
            spread(c, k).wait_recv()
        keep(c).wait()
        for g in range(8):
            y = product(wrow[0, g], wide(got[c, g]))
            hla[2 * g] = wide(y[:K])
            hla[2 * g + 1] = wide(y[K:])
        level(1, wrow.at[1], hla, hlb)
        level(2, wrow.at[2], hlb, hla)
        for j in range(8):
            y = product(wend[j], jnp.concatenate([hla[j], hla[j + 8]], axis=0))
            for half in range(2):
                for m in range(2):
                    r0 = half * LEAF + m * K
                    own[c, m, half * 8 + j] = y[r0 : r0 + K]
        swap(c).start()

        @pl.when(c >= 1)
        def _():
            chain(c - 1, 2)

        @pl.when(c >= 2)
        def _():
            arrive(c - 2)

        begin(c)

        @pl.when(c >= 1)
        def _():
            chain(c - 1, 1)

        @pl.when(c >= 2)
        def _():
            finish(c - 2)

        chain(c, 3)

    chain(C - 1, 2)
    arrive(C - 2)
    chain(C - 1, 1)
    finish(C - 2)
    arrive(C - 1)
    finish(C - 1)

    @pl.loop(0, C)
    def _(c):
        for k in range(len(PEERS)):
            spread(c, k).wait_send()
        swap(c).wait_send()
        for slot in range(7):
            up(c, rp.at[c, slot], slot).wait_send()
            down(c, rm.at[c, slot], slot).wait_send()
        cross(c).wait_send()


def shards(right_sides, leaf_proj, col_levels, middle_factor, row_levels, leaf_expand):
    dma = pltpu.SemaphoreType.DMA
    vmem = pltpu.VMEM
    return pl.pallas_call(
        kernel,
        out_shape=jax.ShapeDtypeStruct((K, R), F32),
        in_specs=[pl.BlockSpec(memory_space=pl.ANY)] * 6,
        out_specs=pl.BlockSpec(memory_space=pltpu.VMEM),
        scratch_shapes=[
            vmem((C, ROWS, W), F32),
            vmem((BOX, K, LEAF), F32),
            vmem((4, 8, LEAF, LEAF), F32),
            vmem((BOX, K, K), F32),
            vmem((4, 8, LEAF, LEAF), F32),
            vmem((BOX, K, LEAF), F32),
            vmem((BOX, K, 2 * LEAF), BF16),
            vmem((4, 8, LEAF, 2 * LEAF), BF16),
            vmem((3, 8, LEAF, 2 * LEAF), BF16),
            vmem((8, 2 * LEAF, 2 * LEAF), BF16),
            vmem((BOX, K, 2 * W), BF16),
            vmem((BOX, K, 2 * W), BF16),
            vmem((C, 8, LEAF, W), F32),
            vmem((C, 8, LEAF, W), F32),
            vmem((C, 2, BOX, K, W), F32),
            vmem((C, BOX, K, W), F32),
            vmem((C, 7, K, W), F32),
            vmem((C, 7, K, W), F32),
            vmem((C, K, W), F32),
            vmem((C, K, W), F32),
            vmem((C, K, W), F32),
            dma((C + 5,)),
            dma((C, 7)),
            dma((C, 7)),
            dma((C,)),
            dma((C,)),
            dma((C,)),
            dma((C, 7)),
            dma((C, 7)),
            dma((C, 7)),
            dma((C, 7)),
            dma((C,)),
            dma((C,)),
        ],
        compiler_params=pltpu.CompilerParams(
            collective_id=0, has_side_effects=True, vmem_limit_bytes=60 * 1024 * 1024
        ),
        name="butterfly",
    )(right_sides, leaf_proj, col_levels, middle_factor, row_levels, jnp.swapaxes(leaf_expand, 2, 3))


def solution(mesh):
    in_specs = (
        P(("tile", "seg"), None),
        P("tile", "seg", None, None),
        P("tile", None, "seg", None, None),
        P("tile", "seg", None, None),
        P("tile", None, "seg", None, None),
        P("tile", "seg", None, None),
    )
    out_specs = P(("seg", "tile"), None)
    return jax.shard_map(shards, mesh=mesh, in_specs=in_specs, out_specs=out_specs, check_vma=False)
```

```python
import functools

import jax
import jax.numpy as jnp
from jax import lax
from jax.experimental import pallas as pl
from jax.experimental.pallas import tpu as pltpu
from jax.sharding import PartitionSpec as P

K = 64
LEAF = 128
BOX = 16
R = 512
C = 4
W = R // C
ROWS = BOX * LEAF
F32 = jnp.float32
BF16 = jnp.bfloat16
MESH = pl.DeviceIdType.MESH
PEERS = ((2, 1), (1, 1), (3, 1), (2, 0), (1, 0), (3, 0), (0, 1))

LATE = 2
TURN = (4, 3, 5, 2, 6, 1, 7, 0)
FIRST = (4, 5)
ORDER = (
    "R0", "B0", "R1", "M0", "B1", "N0", "R2", "M1",
    "A0", "B2", "N1", "F0", "R3", "B3", "M2", "A1",
    "M3", "F1", "F2", "F3",
)


def halves(v):
    hi = v.astype(BF16)
    return hi, (v - hi.astype(F32)).astype(BF16)


def wide(v):
    return jnp.concatenate(halves(v), axis=1)


def product(weight, hl):
    r = jnp.dot(weight, jnp.concatenate([hl, hl], axis=0), preferred_element_type=F32)
    n = r.shape[1] // 2
    return r[:, :n] + r[:, n:]


def exact(a, b):
    hl = wide(b)
    ahi, alo = halves(a)
    r = jnp.dot(ahi, hl, preferred_element_type=F32) + jnp.dot(alo, hl, preferred_element_type=F32)
    n = r.shape[1] // 2
    return r[:, :n] + r[:, n:]


def level(l, weights, src, dst):
    d = 2**l
    for a in range(BOX // (2 * d)):
        for e in range(d):
            p, j = a * 2 * d + e, a * d + e
            y = product(weights[j], jnp.concatenate([src[p], src[p + d]], axis=0))
            dst[p] = wide(y[:K])
            dst[p + d] = wide(y[K:])


def kernel(
    x_hbm, proj_hbm, col_hbm, mid_hbm, row_hbm, exp_hbm, out,
    xbuf, proj, col, mid, row, expt,
    wproj, wcol, wrow, wend, hla, hlb,
    coef, got, own, pair, rp, rm, fin, ysend, yrecv, ends,
    lsem, asend, arecv, csem, dsend, drecv, psend, precv, msend, mrecv, ysems, yrecvs, esend, erecv,
):
    tile, seg = lax.axis_index("tile"), lax.axis_index("seg")
    core, z, yh = tile % 2, (tile // 2) % 8, tile // 16
    xx, yl = seg // 2, seg % 2

    def at(core=core, z=z, yh=yh, xx=xx, yl=yl):
        return ((yh * 8 + z) * 2 + core, xx * 2 + yl)

    other = at(core=1 - core)
    along = {k: at(z=(z + 8 + k) % 8) for k in (1, 2, -1, -2)}
    aside = [at(yh=1 - yh, z=(z + 8 + k) % 8) for k in (1, 2, -1, -2)]
    far = at(yh=1 - yh)
    peers = [at(xx=(xx + dx) % 4, yl=(yl + dy) % 2) for dx, dy in PEERS]

    barrier = pltpu.get_barrier_semaphore()
    friends = peers + [other, far] + list(along.values()) + aside
    for f in friends:
        pl.semaphore_signal(barrier, inc=1, device_id=f, device_id_type=MESH)

    def xcopy(c):
        lanes = pl.ds(pl.multiple_of(c * W, W), W)
        return pltpu.make_async_copy(x_hbm.at[:, lanes], xbuf.at[c], lsem.at[c])

    loads = [
        pltpu.make_async_copy(src, dst, lsem.at[C + i])
        for i, (src, dst) in enumerate(
            [(proj_hbm.at[0], proj), (mid_hbm.at[0], mid), (row_hbm.at[0], row), (exp_hbm.at[0], expt)]
            + [(col_hbm.at[0, l], col.at[l]) for l in range(4)]
        )
    ]
    loads[0].start()
    xcopy(0).start()
    for l in range(4):
        loads[4 + l].start()
    loads[1].start()
    for c in range(1, C):
        xcopy(c).start()
    loads[2].start()
    loads[3].start()

    def remote(src, dst, send, recv, to):
        return pltpu.make_async_remote_copy(
            src_ref=src, dst_ref=dst, send_sem=send, recv_sem=recv, device_id=to, device_id_type=MESH
        )

    def spread(c, k):
        to = peers[k]
        return remote(coef.at[c, to[1]], got.at[c, seg], asend.at[c, k], arecv.at[c, k], to)

    def keep(c):
        return pltpu.make_async_copy(coef.at[c, seg], got.at[c, seg], csem.at[c])

    def swap(c, j):
        two = pl.ds(j * 2, 2)
        return remote(own.at[c, 1 - core, two], pair.at[c, two], dsend.at[c, j], drecv.at[c, j], other)

    def ring(way, c, src, slot, hops=1):
        if way > 0:
            return remote(src, rp.at[c, slot], psend.at[c, slot], precv.at[c, slot], along[hops])
        return remote(src, rm.at[c, slot], msend.at[c, slot], mrecv.at[c, slot], along[-hops])

    def final(c, kind, way, e, src, who=None):
        w = 0 if way > 0 else 1
        who = yh if who is None else who
        b = e if way > 0 else 1 - e
        return remote(
            src, ends.at[c - LATE, kind, w, who], esend.at[c - LATE, kind, w, e], erecv.at[c - LATE, kind, w, who],
            at(yh=b, z=(z + 8 + way * (1 + kind)) % 8),
        )

    def direct(c):
        return remote(own.at[c, core, z * 2 + 1 - yh], yrecv.at[c], ysems.at[c], yrecvs.at[c], far)

    def held(way):
        return rp if way > 0 else rm

    def landed(way, c, slot):
        ring(way, c, held(way).at[c, slot], slot).wait_recv()

    def mine(way, e, off):
        return (z + 8 + way * off) % 8 * 2 + (e if way > 0 else 1 - e)

    def cross(c):
        return remote(ysend.at[c], yrecv.at[c], ysems.at[c], yrecvs.at[c], far)

    def project(c):
        for n in range(BOX):
            hla[n] = wide(product(wproj[n], wide(xbuf[c, n * LEAF : (n + 1) * LEAF])))

    def last(c):
        for j in range(8):
            y = product(wcol[3, j], jnp.concatenate([hlb[j], hlb[j + 8]], axis=0))
            rows = slice((j % 2) * K, (j % 2) * K + K)
            coef[c, j // 2, rows] = y[:K]
            coef[c, j // 2 + 4, rows] = y[K:]

    def send(c):
        for k in range(len(PEERS)):
            spread(c, k).start()

    ping = ((hla, hlb), (hlb, hla), (hla, hlb))
    loads[0].wait()
    for n in range(BOX):
        wproj[n] = wide(proj[n])
    xcopy(0).wait()
    project(0)
    for l in range(3):
        loads[4 + l].wait()
        for j in range(8):
            wcol[l, j] = wide(col[l, j])
        level(l, wcol.at[l], *ping[l])
    loads[7].wait()
    loads[1].wait()
    for j in range(8):
        wcol[3, j, :K] = wide(exact(mid[j], col[3, j, :K]))
        wcol[3, j, K:] = wide(exact(mid[j + 8], col[3, j, K:]))
    last(0)
    pl.semaphore_wait(barrier, len(friends))
    send(0)
    keep(0).start()

    @pl.loop(1, C)
    def _(c):
        xcopy(c).wait()
        project(c)
        for l in range(3):
            level(l, wcol.at[l], *ping[l])
        last(c)
        keep(c).start()

    loads[2].wait()

    @pl.loop(0, 3)
    def _(l):
        for j in range(8):
            wrow[l, j] = wide(row[l, j])

    loads[3].wait()
    for j in range(8):
        wend[j, :LEAF] = wide(exact(expt[j].T, row[3, j, :K]))
        wend[j, LEAF:] = wide(exact(expt[j + 8].T, row[3, j, K:]))

    def begin(c):
        for jj in TURN:
            zz = (z + jj) % 8
            swap(c, zz).wait_recv()
            for b in range(2):
                own[c, core, zz * 2 + b] = own[c, core, zz * 2 + b] + pair[c, zz * 2 + b]
            if jj == 4:
                for way in (1, -1):
                    ring(way, c, own.at[c, core, mine(way, 0, 4)], 0, 2).start()
            if jj in (3, 5):
                way = 4 - jj
                for e in range(2):
                    ring(way, c, own.at[c, core, mine(way, e, 3)], 1 + e).start()
            if c >= LATE and jj in (1, 7):
                way = 1 if jj == 1 else -1
                for e in range(2):
                    final(c, 0, way, e, own.at[c, core, mine(way, e, 1)]).start()
            if c >= LATE and jj == 0:
                direct(c).start()

    def middle(c):
        for e in range(2):
            for way in (1, -1):
                buf = held(way)
                part = own[c, core, mine(way, e, 2)]
                if e == 0:
                    landed(way, c, 0)
                    part = part + buf[c, 0]
                landed(way, c, 1 + e)
                buf[c, 1 + e] = buf[c, 1 + e] + part
                if c >= LATE:
                    final(c, 1, way, e, buf.at[c, 1 + e]).start()
                else:
                    ring(way, c, buf.at[c, 1 + e], 3 + e).start()

    def near(c):
        for e in range(2):
            for way in (1, -1):
                buf = held(way)
                landed(way, c, 3 + e)
                buf[c, 3 + e] = buf[c, 3 + e] + own[c, core, mine(way, e, 1)]
                ring(way, c, buf.at[c, 3 + e], 5 + e).start()

    def arrive(c):
        for e in range(2):
            for way in (1, -1):
                landed(way, c, 5 + e)

        def total(b):
            return own[c, core, z * 2 + b] + rp[c, 5 + b] + rm[c, 6 - b]

        ysend[c] = total(1 - yh)
        cross(c).start()
        fin[c] = total(yh)

    def finish(c):
        if c >= LATE:
            t = own[c, core, z * 2 + yh]
            for kind in range(2):
                for way in (0, 1):
                    for who in range(2):
                        final(c, kind, 1 - 2 * way, 0, ysend.at[c], who).wait_recv()
                        t = t + ends[c - LATE, kind, way, who]
            direct(c).wait_recv()
        else:
            cross(c).wait_recv()
            t = fin[c]
        out[:, c * W : (c + 1) * W] = t + yrecv[c]

    def rows(c):
        for k in FIRST:
            spread(c, k).wait_recv()
        if c + 1 < C:
            send(c + 1)
        for k in range(len(PEERS)):
            if k not in FIRST:
                spread(c, k).wait_recv()
        keep(c).wait()
        for g in range(8):
            y = product(wrow[0, g], wide(got[c, g]))
            hla[2 * g] = wide(y[:K])
            hla[2 * g + 1] = wide(y[K:])
        level(1, wrow.at[1], hla, hlb)
        level(2, wrow.at[2], hlb, hla)
        for jj in TURN:
            j = (z + jj) % 8
            y = product(wend[j], jnp.concatenate([hla[j], hla[j + 8]], axis=0))
            for half in range(2):
                for m in range(2):
                    r0 = half * LEAF + m * K
                    own[c, m, j * 2 + half] = y[r0 : r0 + K]
            swap(c, j).start()

    steps = {
        "R": rows,
        "B": begin,
        "M": middle,
        "N": near,
        "A": arrive,
        "F": finish,
    }
    for step in ORDER:
        steps[step[0]](int(step[1:]))

    @pl.loop(0, C)
    def _(c):
        for k in range(len(PEERS)):
            spread(c, k).wait_send()
        for j in range(8):
            swap(c, j).wait_send()
        for way in (1, -1):
            for slot in range(3):
                ring(way, c, held(way).at[c, slot], slot).wait_send()
        cross(c).wait_send()

    @pl.loop(0, LATE)
    def _(c):
        for way in (1, -1):
            for slot in range(3, 7):
                ring(way, c, held(way).at[c, slot], slot).wait_send()

    @pl.loop(LATE, C)
    def _(c):
        for kind in range(2):
            for way in (1, -1):
                for e in range(2):
                    final(c, kind, way, e, ysend.at[c]).wait_send()


def shards(right_sides, leaf_proj, col_levels, middle_factor, row_levels, leaf_expand):
    dma = pltpu.SemaphoreType.DMA
    vmem = pltpu.VMEM
    return pl.pallas_call(
        kernel,
        out_shape=jax.ShapeDtypeStruct((K, R), F32),
        in_specs=[pl.BlockSpec(memory_space=pl.ANY)] * 6,
        out_specs=pl.BlockSpec(memory_space=pltpu.VMEM),
        scratch_shapes=[
            vmem((C, ROWS, W), F32),
            vmem((BOX, K, LEAF), F32),
            vmem((4, 8, LEAF, LEAF), F32),
            vmem((BOX, K, K), F32),
            vmem((4, 8, LEAF, LEAF), F32),
            vmem((BOX, K, LEAF), F32),
            vmem((BOX, K, 2 * LEAF), BF16),
            vmem((4, 8, LEAF, 2 * LEAF), BF16),
            vmem((3, 8, LEAF, 2 * LEAF), BF16),
            vmem((8, 2 * LEAF, 2 * LEAF), BF16),
            vmem((BOX, K, 2 * W), BF16),
            vmem((BOX, K, 2 * W), BF16),
            vmem((C, 8, LEAF, W), F32),
            vmem((C, 8, LEAF, W), F32),
            vmem((C, 2, BOX, K, W), F32),
            vmem((C, BOX, K, W), F32),
            vmem((C, 7, K, W), F32),
            vmem((C, 7, K, W), F32),
            vmem((C, K, W), F32),
            vmem((C, K, W), F32),
            vmem((C, K, W), F32),
            vmem((C - LATE, 2, 2, 2, K, W), F32),
            dma((C + 8,)),
            dma((C, 7)),
            dma((C, 7)),
            dma((C,)),
            dma((C, 8)),
            dma((C, 8)),
            dma((C, 7)),
            dma((C, 7)),
            dma((C, 7)),
            dma((C, 7)),
            dma((C,)),
            dma((C,)),
            dma((C - LATE, 2, 2, 2)),
            dma((C - LATE, 2, 2, 2)),
        ],
        compiler_params=pltpu.CompilerParams(
            collective_id=0, has_side_effects=True, vmem_limit_bytes=60 * 1024 * 1024
        ),
        name="butterfly",
    )(right_sides, leaf_proj, col_levels, middle_factor, row_levels, jnp.swapaxes(leaf_expand, 2, 3))


def solution(mesh):
    in_specs = (
        P(("tile", "seg"), None),
        P("tile", "seg", None, None),
        P("tile", None, "seg", None, None),
        P("tile", "seg", None, None),
        P("tile", None, "seg", None, None),
        P("tile", "seg", None, None),
    )
    out_specs = P(("seg", "tile"), None)
    return jax.shard_map(shards, mesh=mesh, in_specs=in_specs, out_specs=out_specs, check_vma=False)
```

```python
import functools

import jax
import jax.numpy as jnp
from jax import lax
from jax.experimental import pallas as pl
from jax.experimental.pallas import tpu as pltpu
from jax.sharding import PartitionSpec as P

K = 64
LEAF = 128
BOX = 16
R = 512
C = 4
W = R // C
ROWS = BOX * LEAF
F32 = jnp.float32
BF16 = jnp.bfloat16
MESH = pl.DeviceIdType.MESH
PEERS = ((2, 1), (1, 1), (3, 1), (2, 0), (1, 0), (3, 0), (0, 1))

LATE = 2
TURN = (4, 3, 5, 2, 6, 1, 7, 0)
FIRST = (4, 5, 6)
ORDER = (
    "R0", "B0", "R1", "M0", "B1", "N0", "R2", "M1",
    "A0", "B2", "N1", "F0", "R3", "B3", "M2", "A1",
    "M3", "F1", "F2", "F3",
)


def halves(v):
    hi = v.astype(BF16)
    return hi, (v - hi.astype(F32)).astype(BF16)


def wide(v):
    return jnp.concatenate(halves(v), axis=1)


def product(weight, hl):
    r = jnp.dot(weight, jnp.concatenate([hl, hl], axis=0), preferred_element_type=F32)
    n = r.shape[1] // 2
    return r[:, :n] + r[:, n:]


def exact(a, b):
    hl = wide(b)
    ahi, alo = halves(a)
    r = jnp.dot(ahi, hl, preferred_element_type=F32) + jnp.dot(alo, hl, preferred_element_type=F32)
    n = r.shape[1] // 2
    return r[:, :n] + r[:, n:]


def level(l, weights, src, dst):
    d = 2**l
    for a in range(BOX // (2 * d)):
        for e in range(d):
            p, j = a * 2 * d + e, a * d + e
            y = product(weights[j], jnp.concatenate([src[p], src[p + d]], axis=0))
            dst[p] = wide(y[:K])
            dst[p + d] = wide(y[K:])


def kernel(
    x_hbm, proj_hbm, col_hbm, mid_hbm, row_hbm, exp_hbm, out,
    xbuf, proj, col, mid, row, expt,
    wproj, wcol, wrow, wend, hla, hlb,
    coef, got, own, pair, rp, rm, fin, ysend, yrecv, ends,
    lsem, asend, arecv, csem, dsend, drecv, psend, precv, msend, mrecv, ysems, yrecvs, esend, erecv,
):
    tile, seg = lax.axis_index("tile"), lax.axis_index("seg")
    core, z, yh = tile % 2, (tile // 2) % 8, tile // 16
    xx, yl = seg // 2, seg % 2

    def at(core=core, z=z, yh=yh, xx=xx, yl=yl):
        return ((yh * 8 + z) * 2 + core, xx * 2 + yl)

    other = at(core=1 - core)
    along = {k: at(z=(z + 8 + k) % 8) for k in (1, 2, -1, -2)}
    aside = [at(yh=1 - yh, z=(z + 8 + k) % 8) for k in (1, 2, -1, -2)]
    far = at(yh=1 - yh)
    peers = [at(xx=(xx + dx) % 4, yl=(yl + dy) % 2) for dx, dy in PEERS]

    barrier = pltpu.get_barrier_semaphore()
    friends = peers + [other, far] + list(along.values()) + aside
    for f in friends:
        pl.semaphore_signal(barrier, inc=1, device_id=f, device_id_type=MESH)

    def xcopy(c):
        lanes = pl.ds(pl.multiple_of(c * W, W), W)
        return pltpu.make_async_copy(x_hbm.at[:, lanes], xbuf.at[c], lsem.at[c])

    loads = [
        pltpu.make_async_copy(src, dst, lsem.at[C + i])
        for i, (src, dst) in enumerate(
            [(proj_hbm.at[0], proj), (mid_hbm.at[0], mid), (row_hbm.at[0], row), (exp_hbm.at[0], expt)]
            + [(col_hbm.at[0, l], col.at[l]) for l in range(4)]
        )
    ]
    loads[0].start()
    xcopy(0).start()
    for l in range(4):
        loads[4 + l].start()
    loads[1].start()
    for c in range(1, C):
        xcopy(c).start()
    loads[2].start()
    loads[3].start()

    def remote(src, dst, send, recv, to):
        return pltpu.make_async_remote_copy(
            src_ref=src, dst_ref=dst, send_sem=send, recv_sem=recv, device_id=to, device_id_type=MESH
        )

    def spread(c, k):
        to = peers[k]
        return remote(coef.at[c, to[1]], got.at[c, seg], asend.at[c, k], arecv.at[c, k], to)

    def keep(c):
        return pltpu.make_async_copy(coef.at[c, seg], got.at[c, seg], csem.at[c])

    def swap(c, j):
        two = pl.ds(j * 2, 2)
        return remote(own.at[c, 1 - core, two], pair.at[c, two], dsend.at[c, j], drecv.at[c, j], other)

    def ring(way, c, src, slot, hops=1):
        if way > 0:
            return remote(src, rp.at[c, slot], psend.at[c, slot], precv.at[c, slot], along[hops])
        return remote(src, rm.at[c, slot], msend.at[c, slot], mrecv.at[c, slot], along[-hops])

    def final(c, kind, way, e, src, who=None):
        w = 0 if way > 0 else 1
        who = yh if who is None else who
        b = e if way > 0 else 1 - e
        return remote(
            src, ends.at[c - LATE, kind, w, who], esend.at[c - LATE, kind, w, e], erecv.at[c - LATE, kind, w, who],
            at(yh=b, z=(z + 8 + way * (1 + kind)) % 8),
        )

    def direct(c):
        return remote(own.at[c, core, z * 2 + 1 - yh], yrecv.at[c], ysems.at[c], yrecvs.at[c], far)

    def held(way):
        return rp if way > 0 else rm

    def landed(way, c, slot):
        ring(way, c, held(way).at[c, slot], slot).wait_recv()

    def mine(way, e, off):
        return (z + 8 + way * off) % 8 * 2 + (e if way > 0 else 1 - e)

    def cross(c):
        return remote(ysend.at[c], yrecv.at[c], ysems.at[c], yrecvs.at[c], far)

    def project(c):
        for n in range(BOX):
            hla[n] = wide(product(wproj[n], wide(xbuf[c, n * LEAF : (n + 1) * LEAF])))

    def last(c):
        for j in range(8):
            y = product(wcol[3, j], jnp.concatenate([hlb[j], hlb[j + 8]], axis=0))
            rows = slice((j % 2) * K, (j % 2) * K + K)
            coef[c, j // 2, rows] = y[:K]
            coef[c, j // 2 + 4, rows] = y[K:]

    def send(c):
        for k in range(len(PEERS)):
            spread(c, k).start()

    ping = ((hla, hlb), (hlb, hla), (hla, hlb))
    loads[0].wait()
    for n in range(BOX):
        wproj[n] = wide(proj[n])
    xcopy(0).wait()
    project(0)
    for l in range(3):
        loads[4 + l].wait()
        for j in range(8):
            wcol[l, j] = wide(col[l, j])
        level(l, wcol.at[l], *ping[l])
    loads[7].wait()
    loads[1].wait()
    for j in range(8):
        wcol[3, j, :K] = wide(exact(mid[j], col[3, j, :K]))
        wcol[3, j, K:] = wide(exact(mid[j + 8], col[3, j, K:]))
    last(0)
    pl.semaphore_wait(barrier, len(friends))
    send(0)
    keep(0).start()

    @pl.loop(1, C)
    def _(c):
        xcopy(c).wait()
        project(c)
        for l in range(3):
            level(l, wcol.at[l], *ping[l])
        last(c)
        keep(c).start()

    loads[2].wait()

    @pl.loop(0, 3)
    def _(l):
        for j in range(8):
            wrow[l, j] = wide(row[l, j])

    loads[3].wait()
    for j in range(8):
        wend[j, :LEAF] = wide(exact(expt[j].T, row[3, j, :K]))
        wend[j, LEAF:] = wide(exact(expt[j + 8].T, row[3, j, K:]))

    def begin(c):
        for jj in TURN:
            zz = (z + jj) % 8
            swap(c, zz).wait_recv()
            for b in range(2):
                own[c, core, zz * 2 + b] = own[c, core, zz * 2 + b] + pair[c, zz * 2 + b]
            if jj == 4:
                for way in (1, -1):
                    ring(way, c, own.at[c, core, mine(way, 0, 4)], 0, 2).start()
            if jj in (3, 5):
                way = 4 - jj
                for e in range(2):
                    ring(way, c, own.at[c, core, mine(way, e, 3)], 1 + e).start()
            if c >= LATE and jj in (1, 7):
                way = 1 if jj == 1 else -1
                for e in range(2):
                    final(c, 0, way, e, own.at[c, core, mine(way, e, 1)]).start()
            if c >= LATE and jj == 0:
                direct(c).start()

    def middle(c):
        for e in range(2):
            for way in (1, -1):
                buf = held(way)
                part = own[c, core, mine(way, e, 2)]
                if e == 0:
                    landed(way, c, 0)
                    part = part + buf[c, 0]
                landed(way, c, 1 + e)
                buf[c, 1 + e] = buf[c, 1 + e] + part
                if c >= LATE:
                    final(c, 1, way, e, buf.at[c, 1 + e]).start()
                else:
                    ring(way, c, buf.at[c, 1 + e], 3 + e).start()

    def near(c):
        for e in range(2):
            for way in (1, -1):
                buf = held(way)
                landed(way, c, 3 + e)
                buf[c, 3 + e] = buf[c, 3 + e] + own[c, core, mine(way, e, 1)]
                ring(way, c, buf.at[c, 3 + e], 5 + e).start()

    def arrive(c):
        for e in range(2):
            for way in (1, -1):
                landed(way, c, 5 + e)

        def total(b):
            return own[c, core, z * 2 + b] + rp[c, 5 + b] + rm[c, 6 - b]

        ysend[c] = total(1 - yh)
        cross(c).start()
        fin[c] = total(yh)

    def finish(c):
        if c >= LATE:
            t = own[c, core, z * 2 + yh]
            for kind in range(2):
                for way in (0, 1):
                    for who in range(2):
                        final(c, kind, 1 - 2 * way, 0, ysend.at[c], who).wait_recv()
                        t = t + ends[c - LATE, kind, way, who]
            direct(c).wait_recv()
        else:
            cross(c).wait_recv()
            t = fin[c]
        out[:, c * W : (c + 1) * W] = t + yrecv[c]

    def rows(c):
        for k in FIRST:
            spread(c, k).wait_recv()
        if c + 1 < C:
            send(c + 1)
        for k in range(len(PEERS)):
            if k not in FIRST:
                spread(c, k).wait_recv()
        keep(c).wait()
        for g in range(8):
            y = product(wrow[0, g], wide(got[c, g]))
            hla[2 * g] = wide(y[:K])
            hla[2 * g + 1] = wide(y[K:])
        level(1, wrow.at[1], hla, hlb)
        level(2, wrow.at[2], hlb, hla)
        for jj in TURN:
            j = (z + jj) % 8
            y = product(wend[j], jnp.concatenate([hla[j], hla[j + 8]], axis=0))
            for half in range(2):
                for m in range(2):
                    r0 = half * LEAF + m * K
                    own[c, m, j * 2 + half] = y[r0 : r0 + K]
            swap(c, j).start()

    steps = {
        "R": rows,
        "B": begin,
        "M": middle,
        "N": near,
        "A": arrive,
        "F": finish,
    }
    for step in ORDER:
        steps[step[0]](int(step[1:]))

    @pl.loop(0, C)
    def _(c):
        for k in range(len(PEERS)):
            spread(c, k).wait_send()
        for j in range(8):
            swap(c, j).wait_send()
        for way in (1, -1):
            for slot in range(3):
                ring(way, c, held(way).at[c, slot], slot).wait_send()
        cross(c).wait_send()

    @pl.loop(0, LATE)
    def _(c):
        for way in (1, -1):
            for slot in range(3, 7):
                ring(way, c, held(way).at[c, slot], slot).wait_send()

    @pl.loop(LATE, C)
    def _(c):
        for kind in range(2):
            for way in (1, -1):
                for e in range(2):
                    final(c, kind, way, e, ysend.at[c]).wait_send()


def shards(right_sides, leaf_proj, col_levels, middle_factor, row_levels, leaf_expand):
    dma = pltpu.SemaphoreType.DMA
    vmem = pltpu.VMEM
    return pl.pallas_call(
        kernel,
        out_shape=jax.ShapeDtypeStruct((K, R), F32),
        in_specs=[pl.BlockSpec(memory_space=pl.ANY)] * 6,
        out_specs=pl.BlockSpec(memory_space=pltpu.VMEM),
        scratch_shapes=[
            vmem((C, ROWS, W), F32),
            vmem((BOX, K, LEAF), F32),
            vmem((4, 8, LEAF, LEAF), F32),
            vmem((BOX, K, K), F32),
            vmem((4, 8, LEAF, LEAF), F32),
            vmem((BOX, K, LEAF), F32),
            vmem((BOX, K, 2 * LEAF), BF16),
            vmem((4, 8, LEAF, 2 * LEAF), BF16),
            vmem((3, 8, LEAF, 2 * LEAF), BF16),
            vmem((8, 2 * LEAF, 2 * LEAF), BF16),
            vmem((BOX, K, 2 * W), BF16),
            vmem((BOX, K, 2 * W), BF16),
            vmem((C, 8, LEAF, W), F32),
            vmem((C, 8, LEAF, W), F32),
            vmem((C, 2, BOX, K, W), F32),
            vmem((C, BOX, K, W), F32),
            vmem((C, 7, K, W), F32),
            vmem((C, 7, K, W), F32),
            vmem((C, K, W), F32),
            vmem((C, K, W), F32),
            vmem((C, K, W), F32),
            vmem((C - LATE, 2, 2, 2, K, W), F32),
            dma((C + 8,)),
            dma((C, 7)),
            dma((C, 7)),
            dma((C,)),
            dma((C, 8)),
            dma((C, 8)),
            dma((C, 7)),
            dma((C, 7)),
            dma((C, 7)),
            dma((C, 7)),
            dma((C,)),
            dma((C,)),
            dma((C - LATE, 2, 2, 2)),
            dma((C - LATE, 2, 2, 2)),
        ],
        compiler_params=pltpu.CompilerParams(
            collective_id=0, has_side_effects=True, vmem_limit_bytes=60 * 1024 * 1024
        ),
        name="butterfly",
    )(right_sides, leaf_proj, col_levels, middle_factor, row_levels, jnp.swapaxes(leaf_expand, 2, 3))


def solution(mesh):
    in_specs = (
        P(("tile", "seg"), None),
        P("tile", "seg", None, None),
        P("tile", None, "seg", None, None),
        P("tile", "seg", None, None),
        P("tile", None, "seg", None, None),
        P("tile", "seg", None, None),
    )
    out_specs = P(("seg", "tile"), None)
    return jax.shard_map(shards, mesh=mesh, in_specs=in_specs, out_specs=out_specs, check_vma=False)
```
